32 devices in a mesh: row: 4 (over x, core), col: 8 (over z, y).
Axes of the slice: x: 2, y: 2, z: 4, core: 2. Of those that a mesh axis runs over, the one named last changes fastest.
Arguments:
- object_tiles: float32 [2, 2, 1024, 2048], P(None, None, 'row', 'col'), may hold values from -5 to 5
- probe_modes: float32 [2, 2, 128, 128], replicated, may hold values from -4 to 4
- home_offset: int32 [4, 8, 2, 2], P('row', 'col'), may hold values from 0 to 256
- home_amp: bfloat16 [4, 8, 2, 128, 128], P('row', 'col'), may hold values from 0.19921875 to 1.796875
- sur_offset: int32 [4, 8, 2, 4], P('row', 'col'), may hold values from 0 to 256
- sur_helper: int32 [4, 8, 4], P('row', 'col'), may hold values from -1 to 31, as said below
- help_amp: bfloat16 [4, 8, 4, 128, 128], P('row', 'col'), may hold values from 0.19921875 to 1.796875
Outputs:
- object_grad: float32 [2, 2, 1024, 2048], P(None, None, 'row', 'col')
The draws below stay inside these ranges and needn't reach their ends.
Inputs may be any that keep to these rules, and one draw needn't show every extreme that they name: `sur_helper`: every id that is not -1 is the device at the same tile row and tile column c + 1 or c - 1 (taken modulo 8), as row index times 8 plus column index. No tile sends more than 2 slots to one helper; in every draw some device receives 2 from both column neighbours. The amplitudes of a helper's slots are ordered as in the reference program; slots without a matching surplus position hold values that no output reads.
All inputs are finite; a program needn't handle non-finite values.
Results may differ from the reference program's by a relative error of at most 0.0003.
Values may be sent and summed in bfloat16 or wider, within the bound.
A program may use at most 64 MiB of HBM per device.

```python
import math
import jax
import jax.numpy as jnp
from jax import lax

TILE = 256
MARGIN = 64
WIN = 128
MODES = 2
SLICES = 2
HOME = 2
CAP = 2
SUR = 4
NY = 1024
NX = 2048
N_ROW = 4
N_COL = 8


def draw_sur_helper(key, part):
    keys = jax.random.split(key, 5)
    right_count = jax.random.randint(keys[0], (N_ROW, N_COL), 0, CAP + 1)
    left_count = jax.random.randint(keys[1], (N_ROW, N_COL), 0, CAP + 1)
    sink_row = jax.random.randint(keys[2], (), 0, N_ROW)
    sink_col = jax.random.randint(keys[3], (), 0, N_COL)
    rows_idx = jnp.arange(N_ROW, dtype=jnp.int32)[:, None]
    cols_idx = jnp.arange(N_COL, dtype=jnp.int32)[None, :]
    right_count = jnp.where((rows_idx == sink_row) & (cols_idx == (sink_col - 1) % N_COL), CAP, right_count)
    left_count = jnp.where((rows_idx == sink_row) & (cols_idx == (sink_col + 1) % N_COL), CAP, left_count)
    slot_ids = jnp.arange(SUR, dtype=jnp.int32)[None, None, :]
    code = jnp.where(slot_ids < right_count[:, :, None], 1, jnp.where(slot_ids < (right_count + left_count)[:, :, None], 2, 0))
    perm_keys = jax.random.split(keys[4], N_ROW * N_COL)
    perms = jax.vmap(lambda single: jax.random.permutation(single, SUR))(perm_keys).reshape(N_ROW, N_COL, SUR)
    code = jnp.take_along_axis(code, perms.astype(jnp.int32), axis=-1)
    target_col = jnp.where(code == 1, (cols_idx[:, :, None] + 1) % N_COL, (cols_idx[:, :, None] - 1) % N_COL)
    ids = jnp.where(code == 0, -1, rows_idx[:, :, None] * N_COL + target_col)
    return ids.astype(jnp.int32)


def with_ends(entries, rng, smallest, top_value):
    longest = entries.shape.index(max(entries.shape))
    spots = []
    for shift in (0, 1):
        where = [jax.random.randint(jax.random.fold_in(rng, axis), (), 0, length) for axis, length in enumerate(entries.shape)]
        where[longest] = (where[longest] + shift) % entries.shape[longest]
        spots.append(tuple(where))
    return entries.at[spots[0]].set(smallest).at[spots[1]].set(top_value)


def level_of(stream_key, extent, shards, low, top_value):
    def one(axis_at, shards_of):
        steps = jax.random.uniform(jax.random.fold_in(jax.random.fold_in(stream_key, 6), axis_at), (shards_of,), jnp.float32, low / len(shards), top_value / len(shards))
        return jnp.repeat(jnp.exp(steps), extent[axis_at] // shards_of).reshape((-1,) + (1,) * (len(extent) - axis_at - 1))

    gain = one(*shards[0])
    for cut in shards[1:]:
        gain = gain * one(*cut)
    return gain


def noise(stream_key, shape, deviation, bound, pieces=(), kind=jnp.bfloat16):
    drawn = jax.random.normal(stream_key, shape, jnp.float32) * deviation
    if len(pieces) > 0:
        drawn = level_of(stream_key, shape, pieces, -0.22, 0.18) * drawn
    return jnp.clip(drawn, min=-bound, max=bound).astype(kind)


def setup_inputs(seed: int = 0) -> dict:
    key_list = jax.random.split(jax.random.key(seed), 8)
    return {
        "object_tiles": noise(key_list[0], (2, SLICES, NY, NX), 0.7, 5.0, ((2, 4), (3, 8)), jnp.float32),
        "probe_modes": noise(key_list[1], (2, MODES, WIN, WIN), 0.5, 4.0, (), jnp.float32),
        "home_offset": with_ends(jax.random.randint(key_list[2], (N_ROW, N_COL, 2, HOME), 0, TILE + 2 * MARGIN - WIN + 1), jax.random.fold_in(key_list[2], 1), 0, TILE + 2 * MARGIN - WIN).astype(jnp.int32),
        "home_amp": jnp.clip(0.19921875 + 1.5976562 * jax.random.uniform(key_list[3], (N_ROW, N_COL, HOME, WIN, WIN), jnp.float32) ** level_of(key_list[3], (N_ROW, N_COL, HOME, WIN, WIN), ((0, 4), (1, 8)), -0.2, 0.2), 0.19921875, 1.796875).astype(jnp.bfloat16),
        "sur_offset": with_ends(jax.random.randint(key_list[4], (N_ROW, N_COL, 2, SUR), 0, TILE + 2 * MARGIN - WIN + 1), jax.random.fold_in(key_list[4], 1), 0, TILE + 2 * MARGIN - WIN).astype(jnp.int32),
        "sur_helper": draw_sur_helper(jax.random.fold_in(key_list[7], 71), 0),
        "help_amp": jnp.clip(0.19921875 + 1.5976562 * jax.random.uniform(key_list[6], (N_ROW, N_COL, SUR, WIN, WIN), jnp.float32) ** level_of(key_list[6], (N_ROW, N_COL, SUR, WIN, WIN), ((0, 4), (1, 8)), -0.2, 0.2), 0.19921875, 1.796875).astype(jnp.bfloat16),
    }


smooth_eps = 0.1

def spectral_tables(width):
    index = jnp.arange(width, dtype=jnp.int32)
    product = index[:, None] * index[None, :] % width
    angle = -2.0 * math.pi / width * product.astype(jnp.float32)
    norm_factor = 1.0 / math.sqrt(width)
    freq = (index - width * (index >= width // 2).astype(jnp.int32)).astype(jnp.float32)
    phase = -math.pi / width * (freq[:, None] ** 2 + freq[None, :] ** 2)
    return (jnp.cos(angle) * norm_factor, jnp.sin(angle) * norm_factor, jnp.cos(phase), jnp.sin(phase))

def right_product(left_side, right_side):
    return jnp.matmul(left_side, right_side, precision=lax.Precision.HIGHEST)

def transform(real_part, imag_part, cos_table, sin_table):
    first_real = right_product(real_part, cos_table) - right_product(imag_part, sin_table)
    first_imag = right_product(real_part, sin_table) + right_product(imag_part, cos_table)
    out_real = right_product(cos_table, first_real) - right_product(sin_table, first_imag)
    out_imag = right_product(cos_table, first_imag) + right_product(sin_table, first_real)
    return (out_real, out_imag)

def patch_loss(patch, probe_modes, amplitude, weight, tables):
    cos_table, sin_table, prop_real, prop_imag = tables
    probe_real, probe_imag = (probe_modes[0], probe_modes[1])
    obj_real, obj_imag = (patch[0], patch[1])
    wave_real = probe_real * obj_real[0] - probe_imag * obj_imag[0]
    wave_imag = probe_real * obj_imag[0] + probe_imag * obj_real[0]
    for slice_index in range(1, patch.shape[1]):
        spec_real, spec_imag = transform(wave_real, wave_imag, cos_table, sin_table)
        moved_real = spec_real * prop_real - spec_imag * prop_imag
        moved_imag = spec_real * prop_imag + spec_imag * prop_real
        back_real, back_imag = transform(moved_real, moved_imag, cos_table, -sin_table)
        wave_real = back_real * obj_real[slice_index] - back_imag * obj_imag[slice_index]
        wave_imag = back_real * obj_imag[slice_index] + back_imag * obj_real[slice_index]
    far_real, far_imag = transform(wave_real, wave_imag, cos_table, sin_table)
    intensity = lax.optimization_barrier(jnp.sum(far_real * far_real + far_imag * far_imag, axis=0))
    misfit = jnp.sqrt(intensity + smooth_eps) - amplitude
    return weight * jnp.sum(misfit * misfit)

def reference(object_tiles, probe_modes, home_offset, home_amp, sur_offset, sur_helper, help_amp):
    window = WIN
    tables = spectral_tables(window)
    patch_gradient = jax.vmap(jax.grad(patch_loss), in_axes=(0, None, 0, 0, None))
    row_count = N_ROW
    col_count = N_COL
    tile_rows = jnp.arange(row_count, dtype=jnp.int32)[:, None, None]
    tile_cols = jnp.arange(col_count, dtype=jnp.int32)[None, :, None]
    home_rows = home_offset[:, :, 0, :] + tile_rows * TILE
    home_cols = home_offset[:, :, 1, :] + tile_cols * TILE
    helper_column = sur_helper % col_count
    live = sur_helper >= 0
    to_right = live & (helper_column == (tile_cols + 1) % col_count)
    to_left = live & jnp.logical_not(to_right)
    right_rank = jnp.cumsum(to_right.astype(jnp.int32), axis=-1) - 1
    left_rank = jnp.cumsum(to_left.astype(jnp.int32), axis=-1) - 1
    held_slot = jnp.where(to_right, right_rank, CAP + left_rank)
    held_slot = jnp.where(live, held_slot, 0).astype(jnp.int32)
    held_index = ((tile_rows * col_count + helper_column) * SUR + held_slot).astype(jnp.int32)
    sur_rows = sur_offset[:, :, 0, :] + tile_rows * TILE
    sur_cols = sur_offset[:, :, 1, :] + tile_cols * TILE
    home_total = row_count * col_count * HOME
    all_rows = jnp.concatenate([home_rows.reshape(-1), sur_rows.reshape(-1)]).astype(jnp.int32)
    all_cols = jnp.concatenate([home_cols.reshape(-1), sur_cols.reshape(-1)]).astype(jnp.int32)
    amp_index = jnp.concatenate([jnp.arange(home_total, dtype=jnp.int32), home_total + held_index.reshape(-1)]).astype(jnp.int32)
    live_flag = jnp.concatenate([jnp.ones((home_total,), jnp.int32), live.reshape(-1).astype(jnp.int32)])
    amp_stack = jnp.concatenate([home_amp.reshape(-1, window, window), help_amp.reshape(-1, window, window)], axis=0)
    order = jnp.argsort(1 - live_flag, stable=True).astype(jnp.int32)
    live_count = jnp.sum(live_flag)
    group_len = 16
    order_pad = jnp.concatenate([order, jnp.zeros((group_len,), jnp.int32)])
    weight_pad = jnp.concatenate([live_flag[order], jnp.zeros((group_len,), jnp.int32)]).astype(object_tiles.dtype)
    padded_object = jnp.pad(object_tiles, ((0, 0), (0, 0), (MARGIN, MARGIN), (MARGIN, MARGIN)))
    zero = jnp.zeros((), jnp.int32)

    def one_group(group_index, total):
        start = (group_index * group_len).astype(jnp.int32)
        chosen = lax.dynamic_slice_in_dim(order_pad, start, group_len)
        weights = lax.dynamic_slice_in_dim(weight_pad, start, group_len)
        rows_at = all_rows[chosen]
        cols_at = all_cols[chosen]
        amps = amp_stack[amp_index[chosen]].astype(object_tiles.dtype)

        def cut_one(row_at, col_at):
            return lax.dynamic_slice(padded_object, (zero, zero, row_at, col_at), (2, SLICES, window, window))
        patches = jax.vmap(cut_one)(rows_at, cols_at)
        grads = patch_gradient(patches, probe_modes, amps, weights, tables)

        def add_one(item, acc):
            piece = grads[item]
            current = lax.dynamic_slice(acc, (zero, zero, rows_at[item], cols_at[item]), piece.shape)
            return lax.dynamic_update_slice(acc, current + piece, (zero, zero, rows_at[item], cols_at[item]))
        return lax.fori_loop(0, group_len, add_one, total)
    group_count = (live_count + group_len - 1) // group_len
    grad_padded = lax.fori_loop(0, group_count, one_group, jnp.zeros_like(padded_object))
    return grad_padded[:, :, MARGIN:MARGIN + NY, MARGIN:MARGIN + NX]
```

```python
import math

import numpy as np
import ml_dtypes
import jax
import jax.numpy as jnp
from jax import lax
from jax.experimental import pallas as pl
from jax.experimental.pallas import tpu as pltpu
from jax.sharding import PartitionSpec as P

MARGIN = 64
LANES = 128
EPS = 0.1


def shift_along(block, axis, step):
    size = lax.axis_size(axis)
    pairs = [(i, i + step) for i in range(size) if 0 <= i + step < size]
    return lax.ppermute(block, axis, pairs)


def passed_along(block, axis, distance):
    size = lax.axis_size(axis)
    return lax.ppermute(block, axis, [((i - distance) % size, i) for i in range(size)])


def split_tables(window):
    index = np.arange(window)
    spectral = np.exp(-2j * np.pi / window * (index[:, None] * index[None, :] % window))
    spectral /= math.sqrt(window)
    freq = np.where(index >= window // 2, index - window, index).astype(np.float64)
    carrier = np.exp(-1j * np.pi / window * freq**2)
    propagate = np.conj(spectral) @ (carrier[:, None] * spectral)
    blocks = []
    for table in (propagate, spectral):
        blocks += [table.real, table.imag, -table.imag]
    full = np.stack(blocks).astype(np.float32)
    high = full.astype(ml_dtypes.bfloat16)
    low = (full - high.astype(np.float32)).astype(ml_dtypes.bfloat16)
    return np.stack([high, low])


def split(x):
    high = x.astype(jnp.bfloat16)
    low = (x - high.astype(jnp.float32)).astype(jnp.bfloat16)
    return high, low


def square(tab, which, flip):
    def one(part):
        re, im, neg = (tab[part, 3 * which + k] for k in range(3))
        if flip:
            im, neg = neg, im
        top = jnp.concatenate([re, im], axis=1)
        return jnp.concatenate([top, jnp.concatenate([neg, re], axis=1)], axis=0)

    return one(0), one(1)


def dot(a, b):
    return jnp.dot(a, b, preferred_element_type=jnp.float32)


def sandwich(fields, tab, which, conj):
    rows = [jnp.concatenate([re, im], axis=1) for re, im in fields]
    high, low = split(jnp.concatenate(rows, axis=0))
    t_high, t_low = square(tab, which, conj)
    first = dot(
        jnp.concatenate([high, low, high], axis=1),
        jnp.concatenate([t_high, t_high, t_low], axis=0),
    )
    w = first.shape[1] // 2
    count = len(fields)
    top = jnp.concatenate([first[m * w:(m + 1) * w, :w] for m in range(count)], axis=1)
    low_half = jnp.concatenate([first[m * w:(m + 1) * w, w:] for m in range(count)], axis=1)
    high, low = split(jnp.concatenate([top, low_half], axis=0))
    t_high, t_low = square(tab, which, not conj)
    second = dot(
        jnp.concatenate([t_high, t_low, t_high], axis=1),
        jnp.concatenate([high, high, low], axis=0),
    )
    return [
        (second[:w, m * w:(m + 1) * w], second[w:, m * w:(m + 1) * w]) for m in range(count)
    ]


def times(a, b):
    return a[0] * b[0] - a[1] * b[1], a[0] * b[1] + a[1] * b[0]


def conj_times(a, b):
    return a[0] * b[0] + a[1] * b[1], a[0] * b[1] - a[1] * b[0]


def position_gradient(o1, o2, probes, amp, weight, tab):
    waves = sandwich([times(p, o1) for p in probes], tab, 0, False)
    far = sandwich([times(b, o2) for b in waves], tab, 1, False)
    intensity = sum(re * re + im * im for re, im in far)
    factor = (2.0 * weight) * (1.0 - amp * lax.rsqrt(intensity + EPS))
    exits = sandwich([(re * factor, im * factor) for re, im in far], tab, 1, True)
    g2 = [conj_times(b, e) for b, e in zip(waves, exits)]
    entry = sandwich([conj_times(o2, e) for e in exits], tab, 0, True)
    g1 = [conj_times(p, e) for p, e in zip(probes, entry)]
    total = lambda parts: (sum(p[0] for p in parts), sum(p[1] for p in parts))
    return total(g1), total(g2)


def compute_kernel(
    group, where_ref, weight_ref, tab, probe_ref, amp_ref, ext_ref, out_ref, obj, acc
):
    tiles = ext_ref.shape[2] // LANES
    for p in range(4):
        for q in range(tiles):
            obj[p, q] = ext_ref[p, :, q * LANES:(q + 1) * LANES]
    window = probe_ref.shape[-1]
    modes = probe_ref.shape[1]
    count = where_ref.shape[0]
    lane = lax.broadcasted_iota(jnp.int32, (window, LANES), 1)
    acc[...] = jnp.zeros_like(acc)

    def body(step, carry):
        results = []
        for inner in range(group):
            item = step * group + inner
            row = where_ref[item, 0]
            tile = where_ref[item, 1]
            shift = where_ref[item, 2]
            planes = []
            for p in range(4):
                a = obj[p, tile, pl.ds(row, window), :]
                b = obj[p, tile + 1, pl.ds(row, window), :]
                planes.append(pltpu.roll(jnp.where(lane >= shift, a, b), LANES - shift, 1))
            o1, o2 = (planes[0], planes[2]), (planes[1], planes[3])
            probes = [(probe_ref[0, m], probe_ref[1, m]) for m in range(modes)]
            amp = amp_ref[where_ref[item, 3]].astype(jnp.float32)
            g1, g2 = position_gradient(o1, o2, probes, amp, weight_ref[item], tab)
            results.append((row, tile, shift, (g1[0], g2[0], g1[1], g2[1])))
        for row, tile, shift, grads in results:
            for p in range(4):
                rolled = pltpu.roll(grads[p], shift, 1)
                zero = jnp.zeros_like(rolled)
                here = (p, tile, pl.ds(row, window))
                there = (p, tile + 1, pl.ds(row, window))
                acc[here] = acc[here] + jnp.where(lane >= shift, rolled, zero)
                acc[there] = acc[there] + jnp.where(lane >= shift, zero, rolled)
        return carry

    lax.fori_loop(0, count // group, body, 0)
    for p in range(4):
        for q in range(tiles):
            out_ref[p, :, q * LANES:(q + 1) * LANES] = acc[p, q]


def compute(where, weight, tables, probe_modes, amps, ext):
    vmem = pl.BlockSpec(memory_space=pltpu.VMEM)
    smem = pl.BlockSpec(memory_space=pltpu.SMEM)
    count = where.shape[0]
    group = 2 if count % 2 == 0 else 1
    return pl.pallas_call(
        lambda *refs: compute_kernel(group, *refs),
        out_shape=jax.ShapeDtypeStruct(ext.shape, jnp.float32),
        in_specs=[smem, smem, vmem, vmem, vmem, vmem],
        out_specs=vmem,
        scratch_shapes=[
            pltpu.VMEM((4, ext.shape[2] // LANES, ext.shape[1], LANES), jnp.float32),
            pltpu.VMEM((4, ext.shape[2] // LANES, ext.shape[1], LANES), jnp.float32),
        ],
        compiler_params=pltpu.CompilerParams(vmem_limit_bytes=60 << 20),
        name="positions",
    )(where, weight, tables, probe_modes, amps, ext)


def plan(home_offset, sur_offset, sur_helper, half):
    helper = sur_helper[0, 0]
    columns = lax.axis_size("col")
    my_column = lax.axis_index("col")
    live = helper >= 0
    to_right = live & (helper % columns == (my_column + 1) % columns)
    to_left = live & jnp.logical_not(to_right)
    right_rank = jnp.cumsum(to_right.astype(jnp.int32)) - 1
    left_rank = jnp.cumsum(to_left.astype(jnp.int32)) - 1
    homes = home_offset.shape[3]
    held = jnp.where(to_right, right_rank, half + left_rank)
    held = homes + jnp.where(live, held, 0)
    index = jnp.concatenate([jnp.arange(homes, dtype=jnp.int32), held.astype(jnp.int32)])
    rows = jnp.concatenate([home_offset[0, 0, 0], sur_offset[0, 0, 0]])
    cols = jnp.concatenate([home_offset[0, 0, 1], sur_offset[0, 0, 1]]) + (LANES - MARGIN)
    where = jnp.stack([rows, cols // LANES, cols % LANES, index], axis=1).astype(jnp.int32)
    weight = jnp.concatenate([jnp.ones((homes,), jnp.float32), live.astype(jnp.float32)])
    return where, weight


def shards(object_tiles, probe_modes, home_offset, home_amp, sur_offset, sur_helper, help_amp):
    window = probe_modes.shape[-1]
    tile = object_tiles.shape[-1]
    half = help_amp.shape[2] // 2
    m = MARGIN
    where, weight = plan(home_offset, sur_offset, sur_helper, half)
    amps_right = passed_along(help_amp[0, 0, :half], "col", -1)
    amps_left = passed_along(help_amp[0, 0, half:], "col", 1)
    amps = jnp.concatenate([home_amp[0, 0], amps_right, amps_left], axis=0)
    x = object_tiles.reshape(4, tile, tile)
    up = shift_along(x[:, tile - m:], "row", 1)
    down = shift_along(x[:, :m], "row", -1)
    x = jnp.concatenate([up, x, down], axis=1)
    left = shift_along(x[:, :, tile - m:], "col", 1)
    right = shift_along(x[:, :, :m], "col", -1)
    edge = jnp.zeros(left.shape[:2] + (LANES - m,), jnp.float32)
    ext = jnp.concatenate([edge, left, x, right, edge], axis=2)
    grad = compute(where, weight, jnp.asarray(split_tables(window)), probe_modes, amps, ext)
    to_left = shift_along(grad[:, :, LANES - m:LANES], "col", -1)
    to_right = shift_along(grad[:, :, LANES + tile:LANES + tile + m], "col", 1)
    center = grad[:, :, LANES:LANES + tile]
    center = jnp.concatenate(
        [center[:, :, :m] + to_right, center[:, :, m:tile - m], center[:, :, tile - m:] + to_left],
        axis=2,
    )
    to_up = shift_along(center[:, :m], "row", -1)
    to_down = shift_along(center[:, m + tile:], "row", 1)
    center = center[:, m:m + tile]
    center = jnp.concatenate(
        [center[:, :m] + to_down, center[:, m:tile - m], center[:, tile - m:] + to_up], axis=1
    )
    return center.reshape(object_tiles.shape)


def solution(mesh):
    return jax.shard_map(
        shards,
        mesh=mesh,
        in_specs=(
            P(None, None, "row", "col"),
            P(),
            P("row", "col", None, None),
            P("row", "col", None, None, None),
            P("row", "col", None, None),
            P("row", "col", None),
            P("row", "col", None, None, None),
        ),
        out_specs=P(None, None, "row", "col"),
        check_vma=False,
    )
```

```python
import functools
import math

import numpy as np
import ml_dtypes
import jax
import jax.numpy as jnp
from jax import lax
from jax.experimental import pallas as pl
from jax.experimental.pallas import tpu as pltpu
from jax.sharding import PartitionSpec as P

MARGIN = 64
LANES = 128
EPS = 0.1
MESH = pl.DeviceIdType.MESH
SIDES = ((1, 0), (-1, 0), (0, 1), (0, -1), (1, 1), (-1, 1), (1, -1), (-1, -1))


def split_tables(window):
    index = np.arange(window)
    spectral = np.exp(-2j * np.pi / window * (index[:, None] * index[None, :] % window))
    spectral /= math.sqrt(window)
    freq = np.where(index >= window // 2, index - window, index).astype(np.float64)
    carrier = np.exp(-1j * np.pi / window * freq**2)
    propagate = np.conj(spectral) @ (carrier[:, None] * spectral)
    blocks = []
    for table in (propagate, spectral):
        blocks += [table.real, table.imag, -table.imag]
    full = np.stack(blocks).astype(np.float32)
    high = full.astype(ml_dtypes.bfloat16)
    low = (full - high.astype(np.float32)).astype(ml_dtypes.bfloat16)
    return np.stack([high, low])


def split(x):
    high = x.astype(jnp.bfloat16)
    low = (x - high.astype(jnp.float32)).astype(jnp.bfloat16)
    return high, low


def square(tab, which, flip):
    def one(part):
        re, im, neg = (tab[part, 3 * which + k] for k in range(3))
        if flip:
            im, neg = neg, im
        top = jnp.concatenate([re, im], axis=1)
        return jnp.concatenate([top, jnp.concatenate([neg, re], axis=1)], axis=0)

    return one(0), one(1)


def dot(a, b):
    return jnp.dot(a, b, preferred_element_type=jnp.float32)


def sandwich(fields, tab, which, conj):
    rows = [jnp.concatenate([re, im], axis=1) for re, im in fields]
    high, low = split(jnp.concatenate(rows, axis=0))
    t_high, t_low = square(tab, which, conj)
    first = dot(
        jnp.concatenate([high, low, high], axis=1),
        jnp.concatenate([t_high, t_high, t_low], axis=0),
    )
    w = first.shape[1] // 2
    count = len(fields)
    top = jnp.concatenate([first[m * w:(m + 1) * w, :w] for m in range(count)], axis=1)
    low_half = jnp.concatenate([first[m * w:(m + 1) * w, w:] for m in range(count)], axis=1)
    high, low = split(jnp.concatenate([top, low_half], axis=0))
    t_high, t_low = square(tab, which, not conj)
    second = dot(
        jnp.concatenate([t_high, t_low, t_high], axis=1),
        jnp.concatenate([high, high, low], axis=0),
    )
    return [
        (second[:w, m * w:(m + 1) * w], second[w:, m * w:(m + 1) * w]) for m in range(count)
    ]


def times(a, b):
    return a[0] * b[0] - a[1] * b[1], a[0] * b[1] + a[1] * b[0]


def conj_times(a, b):
    return a[0] * b[0] + a[1] * b[1], a[0] * b[1] - a[1] * b[0]


def lanes(shape):
    return lax.broadcasted_iota(jnp.int32, shape, len(shape) - 1)


def pair_up(re, im, keep_high):
    half = LANES // 2
    if keep_high:
        return jnp.where(lanes(re.shape) < half, pltpu.roll(re, half, 1), im)
    return jnp.where(lanes(re.shape) < half, re, pltpu.roll(im, half, 1))


def kernel(
    grid_shape, home_off, sur_off, helper_ref, tab, probe_ref, x_ref, home_amp, help_amp, out_ref,
    meta, obj0, obj1, acc, pack, side, gpack, grow, gside, gcorner, amps, waves, patches,
    send_sem, recv_sem, amp_send, amp_recv,
):
    n_row, n_col = grid_shape
    obj = (obj0, obj1)
    row, col = lax.axis_index("row"), lax.axis_index("col")
    tile = x_ref.shape[2]
    window = probe_ref.shape[-1]
    modes = probe_ref.shape[1]
    homes = home_amp.shape[0]
    slots = help_amp.shape[0]
    half = slots // 2
    count = homes + slots
    m = MARGIN
    ext = tile + 2 * m
    tiles = obj0.shape[1]
    inner = tile // LANES

    def inside(dr, dc):
        r, c = row + dr, col + dc
        return (r >= 0) & (r < n_row) & (c >= 0) & (c < n_col)

    ring = [(row, lax.rem(col + 1, n_col)), (row, lax.rem(col + n_col - 1, n_col))]
    barrier = pltpu.get_barrier_semaphore()
    for target in ring:
        pl.semaphore_signal(barrier, inc=1, device_id=target, device_id_type=MESH)
    for dr, dc in SIDES:
        if dr != 0:
            @pl.when(inside(dr, dc))
            def _(dr=dr, dc=dc):
                pl.semaphore_signal(
                    barrier, inc=1, device_id=(row + dr, col + dc), device_id_type=MESH
                )

    for k in range(2):
        first, last = x_ref[:, k, :, 0:LANES], x_ref[:, k, :, tile - LANES:tile]
        pack[k, 0] = pair_up(first[0], first[1], False)
        pack[k, 1] = pair_up(last[0], last[1], True)

    vertical = jnp.where(row > 0, 1, 0) + jnp.where(row + 1 < n_row, 1, 0)
    across = 1 + jnp.where(col > 0, 1, 0) + jnp.where(col + 1 < n_col, 1, 0)
    pl.semaphore_wait(barrier, 2 + vertical * across)

    def remote(src, dst, phase, k, index, target):
        return pltpu.make_async_remote_copy(
            src_ref=src, dst_ref=dst,
            send_sem=send_sem.at[phase, k, index], recv_sem=recv_sem.at[phase, k, index],
            device_id=target, device_id_type=MESH,
        )

    def edge(d, source):
        if d == 0:
            return slice(m, m + tile) if source == "ext" else slice(0, tile)
        if source == "ext":
            return slice(ext - m, ext) if d > 0 else slice(0, m)
        return slice(tile - m, tile) if d > 0 else slice(0, m)

    def halo_copies(n, k):
        dr, dc = SIDES[n]
        target = (row + dr, col + dc)
        landing = edge(-dr, "ext")
        if dc == 0:
            return [
                remote(
                    x_ref.at[:, k, edge(dr, "tile"), q * LANES:(q + 1) * LANES],
                    obj[k].at[:, 1 + q, landing, :], 0, k, n + 8 * q, target,
                )
                for q in range(inner)
            ]
        s = 1 if dc > 0 else 0
        return [remote(pack.at[k, s, edge(dr, "tile")], side.at[k, 1 - s, landing], 0, k, n, target)]

    def grad_copies(n, k):
        dr, dc = SIDES[n]
        target = (row + dr, col + dc)
        take = edge(dr, "ext")
        if dc == 0:
            u = 1 if dr > 0 else 0
            return [remote(acc.at[:, k, 1:1 + inner, take, :], grow.at[k, 1 - u], 1, k, n, target)]
        s = 1 if dc > 0 else 0
        source = gpack.at[k, s, take]
        if dr == 0:
            return [remote(source, gside.at[k, 1 - s], 1, k, n, target)]
        u = 1 if dr > 0 else 0
        return [remote(source, gcorner.at[k, 1 - s, 1 - u], 1, k, n, target)]

    def start(copies, k):
        for n, (dr, dc) in sorted(enumerate(SIDES), key=lambda e: e[1][1] == 0):
            @pl.when(inside(dr, dc))
            def _(n=n):
                for copy in copies(n, k):
                    copy.start()

    def wait_recv(copies, k):
        for n, (dr, dc) in enumerate(SIDES):
            @pl.when(inside(-dr, -dc))
            def _(n=n):
                for copy in copies(n, k):
                    copy.wait_recv()

    def wait_send(copies, k):
        for n, (dr, dc) in enumerate(SIDES):
            @pl.when(inside(dr, dc))
            def _(n=n):
                for copy in copies(n, k):
                    copy.wait_send()

    start(halo_copies, 0)
    start(halo_copies, 1)
    amp_copies = [
        pltpu.make_async_remote_copy(
            src_ref=help_amp.at[h * half:(h + 1) * half],
            dst_ref=amps.at[homes + h * half:homes + (h + 1) * half],
            send_sem=amp_send.at[h], recv_sem=amp_recv.at[h],
            device_id=ring[1 - h], device_id_type=MESH,
        )
        for h in range(2)
    ]
    for copy in amp_copies:
        copy.start()

    for n, (dr, dc) in enumerate(SIDES):
        @pl.when(jnp.logical_not(inside(-dr, -dc)))
        def _(dr=dr, dc=dc):
            landing = edge(-dr, "ext")
            u = 1 if dr > 0 else 0
            s = 1 if dc > 0 else 0
            for k in range(2):
                if dc == 0:
                    halo = obj[k][:, 1:1 + inner, landing, :]
                    obj[k][:, 1:1 + inner, landing, :] = jnp.zeros(halo.shape, jnp.float32)
                    grow[k, 1 - u] = jnp.zeros(grow.shape[2:], jnp.float32)
                else:
                    rows_here = landing.stop - landing.start
                    side[k, 1 - s, landing] = jnp.zeros((rows_here, LANES), jnp.float32)
                    if dr == 0:
                        gside[k, 1 - s] = jnp.zeros(gside.shape[2:], jnp.float32)
                    else:
                        gcorner[k, 1 - s, 1 - u] = jnp.zeros(gcorner.shape[3:], jnp.float32)

    for h in range(homes):
        c = home_off[1, h] + (LANES - m)
        for at, value in enumerate((home_off[0, h], lax.div(c, LANES), lax.rem(c, LANES), h, 1)):
            meta[h, at] = jnp.int32(value)
    next_column = lax.rem(col + 1, n_col)
    rights, lefts = jnp.int32(0), jnp.int32(0)
    for h in range(slots):
        helper = helper_ref[h]
        live = jnp.where(helper >= 0, 1, 0)
        right = jnp.where(lax.rem(jnp.maximum(helper, 0), n_col) == next_column, live, 0)
        left = live - right
        held = jnp.minimum(right * rights + left * (half + lefts), slots - 1)
        rights, lefts = rights + right, lefts + left
        c = sur_off[1, h] + (LANES - m)
        values = (sur_off[0, h], lax.div(c, LANES), lax.rem(c, LANES), homes + held, live)
        for at, value in enumerate(values):
            meta[homes + h, at] = value

    for a in range(2):
        for k in range(2):
            for q in range(inner):
                obj[k][a, 1 + q, m:m + tile, :] = x_ref[a, k, :, q * LANES:(q + 1) * LANES]
    amps[0:homes] = home_amp[...]
    patches[...] = jnp.zeros_like(patches)

    def unpack(k):
        wait_recv(halo_copies, k)
        lower, upper = side[k, 0], side[k, 1]
        obj[k][0, 0] = pltpu.roll(lower, LANES // 2, 1)
        obj[k][1, 0] = lower
        obj[k][0, tiles - 1] = upper
        obj[k][1, tiles - 1] = pltpu.roll(upper, LANES // 2, 1)

    lane = lanes((window, LANES))

    def cut(item, k):
        at, q, shift = meta[item, 0], meta[item, 1], meta[item, 2]
        out = []
        for a in range(2):
            here = obj[k][a, q, pl.ds(at, window), :]
            there = obj[k][a, q + 1, pl.ds(at, window), :]
            out.append(pltpu.roll(jnp.where(lane >= shift, here, there), LANES - shift, 1))
        return tuple(out)

    def put(item, grad):
        shift = meta[item, 2]
        for a in range(2):
            patches[item, a, tile:tile + window, :] = pltpu.roll(grad[a], shift, 1)

    def total(parts):
        return sum(p[0] for p in parts), sum(p[1] for p in parts)

    probes = lambda: [(probe_ref[0, j], probe_ref[1, j]) for j in range(modes)]
    kept = lambda item: [(waves[item, j, 0], waves[item, j, 1]) for j in range(modes)]

    def keep(item, fields):
        for j, (re, im) in enumerate(fields):
            waves[item, j, 0] = re
            waves[item, j, 1] = im

    def each(fn):
        def step(i, carry):
            for j in range(GROUP):
                fn(i * GROUP + j)
            return carry

        lax.fori_loop(0, count // GROUP, step, 0)

    def enter(item):
        o1 = cut(item, 0)
        keep(item, sandwich([times(p, o1) for p in probes()], tab, 0, False))

    def middle(item):
        o2 = cut(item, 1)
        fields = kept(item)
        far = sandwich([times(b, o2) for b in fields], tab, 1, False)
        intensity = sum(re * re + im * im for re, im in far)
        amp = amps[meta[item, 3]].astype(jnp.float32)
        weight = 2.0 * meta[item, 4].astype(jnp.float32)
        factor = weight * (1.0 - amp * lax.rsqrt(intensity + EPS))
        exits = sandwich([(re * factor, im * factor) for re, im in far], tab, 1, True)
        put(item, total([conj_times(b, e) for b, e in zip(fields, exits)]))
        keep(item, [conj_times(o2, e) for e in exits])

    def leave(item):
        entry = sandwich(kept(item), tab, 0, True)
        put(item, total([conj_times(p, e) for p, e in zip(probes(), entry)]))

    chunk = 32

    def gather(k):
        lane8 = lanes((chunk, LANES))

        def step(i, carry):
            begin = pl.multiple_of(i * chunk, chunk)
            for a in range(2):
                sums = [jnp.zeros((chunk, LANES), jnp.float32) for _ in range(tiles)]
                for item in range(count):
                    at, q, shift = meta[item, 0], meta[item, 1], meta[item, 2]
                    piece = patches[item, a, pl.ds(tile - at + begin, chunk), :]
                    high = jnp.where(lane8 >= shift, piece, 0.0)
                    low = piece - high
                    for t in range(tiles):
                        hit = jnp.where(q == t, 1.0, 0.0)
                        miss = jnp.where(q + 1 == t, 1.0, 0.0)
                        sums[t] = sums[t] + (high * hit + low * miss)
                for t in range(tiles):
                    acc[a, k, t, pl.ds(begin, chunk), :] = sums[t]
            return carry

        lax.fori_loop(0, ext // chunk, step, 0)
        gpack[k, 0] = pair_up(acc[0, k, 0], acc[1, k, 0], True)
        gpack[k, 1] = pair_up(acc[0, k, tiles - 1], acc[1, k, tiles - 1], False)
        start(grad_copies, k)

    def finish(k):
        wait_recv(grad_copies, k)
        low = lanes((tile, LANES)) < LANES // 2
        for q in range(inner):
            for a in range(2):
                value = acc[a, k, 1 + q, m:m + tile, :]
                top = value[:m] + grow[k, 0, a, q]
                bottom = value[tile - m:] + grow[k, 1, a, q]
                value = jnp.concatenate([top, value[m:tile - m], bottom], axis=0)
                for s in range(2):
                    if (s == 0 and q != 0) or (s == 1 and q != inner - 1):
                        continue
                    extra = gside[k, s]
                    extra = jnp.concatenate(
                        [
                            extra[:m] + gcorner[k, s, 0],
                            extra[m:tile - m],
                            extra[tile - m:] + gcorner[k, s, 1],
                        ],
                        axis=0,
                    )
                    if a != s:
                        extra = pltpu.roll(extra, LANES // 2, 1)
                    value = value + jnp.where(low if s == 0 else jnp.logical_not(low), extra, 0.0)
                out_ref[a, k, :, q * LANES:(q + 1) * LANES] = value

    unpack(0)
    each(enter)
    unpack(1)
    for copy in amp_copies:
        copy.wait_recv()
    each(middle)
    gather(1)
    each(leave)
    gather(0)
    finish(1)
    finish(0)
    for k in range(2):
        wait_send(halo_copies, k)
        wait_send(grad_copies, k)
    for copy in amp_copies:
        copy.wait_send()


GROUP = 2


def shards(object_tiles, probe_modes, home_offset, home_amp, sur_offset, sur_helper, help_amp):
    window = probe_modes.shape[-1]
    modes = probe_modes.shape[1]
    tile = object_tiles.shape[-1]
    ext = tile + 2 * MARGIN
    tiles = tile // LANES + 2
    inner = tile // LANES
    count = home_amp.shape[2] + help_amp.shape[2]
    grid_shape = (lax.axis_size("row"), lax.axis_size("col"))
    vmem = pl.BlockSpec(memory_space=pltpu.VMEM)
    smem = pl.BlockSpec(memory_space=pltpu.SMEM)
    f32 = jnp.float32
    return pl.pallas_call(
        functools.partial(kernel, grid_shape),
        out_shape=jax.ShapeDtypeStruct(object_tiles.shape, f32),
        in_specs=[smem] * 3 + [vmem] * 5,
        out_specs=vmem,
        scratch_shapes=[
            pltpu.SMEM((count, 5), jnp.int32),
            pltpu.VMEM((2, tiles, ext, LANES), f32),
            pltpu.VMEM((2, tiles, ext, LANES), f32),
            pltpu.VMEM((2, 2, tiles, ext, LANES), f32),
            pltpu.VMEM((2, 2, tile, LANES), f32),
            pltpu.VMEM((2, 2, ext, LANES), f32),
            pltpu.VMEM((2, 2, ext, LANES), f32),
            pltpu.VMEM((2, 2, 2, inner, MARGIN, LANES), f32),
            pltpu.VMEM((2, 2, tile, LANES), f32),
            pltpu.VMEM((2, 2, 2, MARGIN, LANES), f32),
            pltpu.VMEM((count, window, window), jnp.bfloat16),
            pltpu.VMEM((count, modes, 2, window, window), f32),
            pltpu.VMEM((count, 2, 2 * tile + window, LANES), f32),
            pltpu.SemaphoreType.DMA((2, 2, 8 + 8 * (inner - 1))),
            pltpu.SemaphoreType.DMA((2, 2, 8 + 8 * (inner - 1))),
            pltpu.SemaphoreType.DMA((2,)),
            pltpu.SemaphoreType.DMA((2,)),
        ],
        compiler_params=pltpu.CompilerParams(
            collective_id=0, has_side_effects=True, vmem_limit_bytes=60 << 20
        ),
        name="multislice",
    )(
        home_offset[0, 0], sur_offset[0, 0], sur_helper[0, 0],
        jnp.asarray(split_tables(window)), probe_modes, object_tiles, home_amp[0, 0], help_amp[0, 0],
    )


def solution(mesh):
    return jax.shard_map(
        shards,
        mesh=mesh,
        in_specs=(
            P(None, None, "row", "col"),
            P(),
            P("row", "col", None, None),
            P("row", "col", None, None, None),
            P("row", "col", None, None),
            P("row", "col", None),
            P("row", "col", None, None, None),
        ),
        out_specs=P(None, None, "row", "col"),
        check_vma=False,
    )
```

```python
import functools
import math

import numpy as np
import ml_dtypes
import jax
import jax.numpy as jnp
from jax import lax
from jax.experimental import pallas as pl
from jax.experimental.pallas import tpu as pltpu
from jax.sharding import PartitionSpec as P

MARGIN = 64
LANES = 128
EPS = 0.1
LEVELS = 32766.0
TINY = 1e-30
MESH = pl.DeviceIdType.MESH
SIDES = ((1, 0), (-1, 0), (0, 1), (0, -1), (1, 1), (-1, 1), (1, -1), (-1, -1))


def split_tables(window):
    index = np.arange(window)
    spectral = np.exp(-2j * np.pi / window * (index[:, None] * index[None, :] % window))
    spectral /= math.sqrt(window)
    freq = np.where(index >= window // 2, index - window, index).astype(np.float64)
    carrier = np.exp(-1j * np.pi / window * freq**2)
    propagate = np.conj(spectral) @ (carrier[:, None] * spectral)
    blocks = []
    for table in (propagate, spectral):
        blocks += [table.real, table.imag, -table.imag]
    full = np.stack(blocks).astype(np.float32)
    high = full.astype(ml_dtypes.bfloat16)
    low = (full - high.astype(np.float32)).astype(ml_dtypes.bfloat16)
    return np.stack([high, low])


def split(x):
    high = x.astype(jnp.bfloat16)
    low = (x - high.astype(jnp.float32)).astype(jnp.bfloat16)
    return high, low


def square(tab, which, flip):
    def one(part):
        re, im, neg = (tab[part, 3 * which + k] for k in range(3))
        if flip:
            im, neg = neg, im
        top = jnp.concatenate([re, im], axis=1)
        return jnp.concatenate([top, jnp.concatenate([neg, re], axis=1)], axis=0)

    return one(0), one(1)


def dot(a, b):
    return jnp.dot(a, b, preferred_element_type=jnp.float32)


def sandwich(fields, tab, which, conj):
    rows = [jnp.concatenate([re, im], axis=1) for re, im in fields]
    high, low = split(jnp.concatenate(rows, axis=0))
    t_high, t_low = square(tab, which, conj)
    first = dot(
        jnp.concatenate([high, low, high], axis=1),
        jnp.concatenate([t_high, t_high, t_low], axis=0),
    )
    w = first.shape[1] // 2
    count = len(fields)
    top = jnp.concatenate([first[m * w:(m + 1) * w, :w] for m in range(count)], axis=1)
    low_half = jnp.concatenate([first[m * w:(m + 1) * w, w:] for m in range(count)], axis=1)
    high, low = split(jnp.concatenate([top, low_half], axis=0))
    t_high, t_low = square(tab, which, not conj)
    second = dot(
        jnp.concatenate([t_high, t_low, t_high], axis=1),
        jnp.concatenate([high, high, low], axis=0),
    )
    return [
        (second[:w, m * w:(m + 1) * w], second[w:, m * w:(m + 1) * w]) for m in range(count)
    ]


def times(a, b):
    return a[0] * b[0] - a[1] * b[1], a[0] * b[1] + a[1] * b[0]


def conj_times(a, b):
    return a[0] * b[0] + a[1] * b[1], a[0] * b[1] - a[1] * b[0]


def lanes(shape):
    return lax.broadcasted_iota(jnp.int32, shape, len(shape) - 1)


def pair_up(re, im, keep_high):
    half = LANES // 2
    if keep_high:
        return jnp.where(lanes(re.shape) < half, pltpu.roll(re, half, 1), im)
    return jnp.where(lanes(re.shape) < half, re, pltpu.roll(im, half, 1))


def kernel(
    grid_shape, home_off, sur_off, helper_ref, tab, probe_ref, x_ref, home_amp, help_amp, out_ref,
    meta, obj0, obj1, acc, pack, side, gpack, grow, gside, gcorner, scale_out, scale_in, amps, waves, patches,
    send_sem, recv_sem, amp_send, amp_recv,
):
    n_row, n_col = grid_shape
    obj = (obj0, obj1)
    row, col = lax.axis_index("row"), lax.axis_index("col")
    tile = x_ref.shape[2]
    window = probe_ref.shape[-1]
    modes = probe_ref.shape[1]
    homes = home_amp.shape[0]
    slots = help_amp.shape[0]
    half = slots // 2
    count = homes + slots
    m = MARGIN
    ext = tile + 2 * m
    tiles = obj0.shape[1]
    inner = tile // LANES

    def inside(dr, dc):
        r, c = row + dr, col + dc
        return (r >= 0) & (r < n_row) & (c >= 0) & (c < n_col)

    ring = [(row, lax.rem(col + 1, n_col)), (row, lax.rem(col + n_col - 1, n_col))]
    barrier = pltpu.get_barrier_semaphore()
    for target in ring:
        pl.semaphore_signal(barrier, inc=1, device_id=target, device_id_type=MESH)
    for dr, dc in SIDES:
        if dr != 0:
            @pl.when(inside(dr, dc))
            def _(dr=dr, dc=dc):
                pl.semaphore_signal(
                    barrier, inc=1, device_id=(row + dr, col + dc), device_id_type=MESH
                )

    def encode(target, phase, k, strips):
        top = functools.reduce(
            jnp.maximum, [jnp.max(jnp.abs(v), axis=(0, 1), keepdims=True) for v in strips]
        )
        top = jnp.maximum(top, TINY)
        for s, v in enumerate(strips):
            target[k, s] = jnp.round(v * (LEVELS / top)).astype(jnp.int32).astype(jnp.int16)
        scale_out[phase, k] = jnp.broadcast_to(top * (1.0 / LEVELS), scale_out.shape[2:])

    def decode(value, phase, k, n):
        return value.astype(jnp.int32).astype(jnp.float32) * scale_in[phase, k, n - 2, 0:1, :]

    for k in range(2):
        first, last = x_ref[:, k, :, 0:LANES], x_ref[:, k, :, tile - LANES:tile]
        encode(pack, 0, k, [pair_up(first[0], first[1], False), pair_up(last[0], last[1], True)])

    vertical = jnp.where(row > 0, 1, 0) + jnp.where(row + 1 < n_row, 1, 0)
    across = 1 + jnp.where(col > 0, 1, 0) + jnp.where(col + 1 < n_col, 1, 0)
    pl.semaphore_wait(barrier, 2 + vertical * across)

    def remote(src, dst, phase, k, index, target):
        return pltpu.make_async_remote_copy(
            src_ref=src, dst_ref=dst,
            send_sem=send_sem.at[phase, k, index], recv_sem=recv_sem.at[phase, k, index],
            device_id=target, device_id_type=MESH,
        )

    def edge(d, source):
        if d == 0:
            return slice(m, m + tile) if source == "ext" else slice(0, tile)
        if source == "ext":
            return slice(ext - m, ext) if d > 0 else slice(0, m)
        return slice(tile - m, tile) if d > 0 else slice(0, m)

    def scale_copy(phase, k, n, target):
        return remote(
            scale_out.at[phase, k], scale_in.at[phase, k, n - 2], phase, k, 8 * inner + n, target
        )

    def halo_copies(n, k):
        dr, dc = SIDES[n]
        target = (row + dr, col + dc)
        landing = edge(-dr, "ext")
        if dc == 0:
            return [
                remote(
                    x_ref.at[:, k, edge(dr, "tile"), q * LANES:(q + 1) * LANES],
                    obj[k].at[:, 1 + q, landing, :], 0, k, n + 8 * q, target,
                )
                for q in range(inner)
            ]
        s = 1 if dc > 0 else 0
        return [
            remote(pack.at[k, s, edge(dr, "tile")], side.at[k, 1 - s, landing], 0, k, n, target),
            scale_copy(0, k, n, target),
        ]

    def grad_copies(n, k):
        dr, dc = SIDES[n]
        target = (row + dr, col + dc)
        take = edge(dr, "ext")
        if dc == 0:
            u = 1 if dr > 0 else 0
            return [remote(acc.at[:, k, 1:1 + inner, take, :], grow.at[k, 1 - u], 1, k, n, target)]
        s = 1 if dc > 0 else 0
        source = gpack.at[k, s, take]
        if dr == 0:
            landing = gside.at[k, 1 - s]
        else:
            landing = gcorner.at[k, 1 - s, 0 if dr > 0 else 1]
        return [remote(source, landing, 1, k, n, target), scale_copy(1, k, n, target)]

    def start(copies, k):
        for n, (dr, dc) in sorted(enumerate(SIDES), key=lambda e: e[1][1] == 0):
            @pl.when(inside(dr, dc))
            def _(n=n):
                for copy in copies(n, k):
                    copy.start()

    def wait_recv(copies, k):
        for n, (dr, dc) in enumerate(SIDES):
            @pl.when(inside(-dr, -dc))
            def _(n=n):
                for copy in copies(n, k):
                    copy.wait_recv()

    def wait_send(copies, k):
        for n, (dr, dc) in enumerate(SIDES):
            @pl.when(inside(dr, dc))
            def _(n=n):
                for copy in copies(n, k):
                    copy.wait_send()

    start(halo_copies, 0)
    start(halo_copies, 1)
    amp_copies = [
        pltpu.make_async_remote_copy(
            src_ref=help_amp.at[h * half:(h + 1) * half],
            dst_ref=amps.at[h * half:(h + 1) * half],
            send_sem=amp_send.at[h], recv_sem=amp_recv.at[h],
            device_id=ring[1 - h], device_id_type=MESH,
        )
        for h in range(2)
    ]
    for copy in amp_copies:
        copy.start()

    for n, (dr, dc) in enumerate(SIDES):
        @pl.when(jnp.logical_not(inside(-dr, -dc)))
        def _(n=n, dr=dr, dc=dc):
            landing = edge(-dr, "ext")
            u = 1 if dr > 0 else 0
            s = 1 if dc > 0 else 0
            for k in range(2):
                if dc == 0:
                    halo = obj[k][:, 1:1 + inner, landing, :]
                    obj[k][:, 1:1 + inner, landing, :] = jnp.zeros(halo.shape, jnp.float32)
                    grow[k, 1 - u] = jnp.zeros(grow.shape[2:], jnp.float32)
                else:
                    rows_here = landing.stop - landing.start
                    side[k, 1 - s, landing] = jnp.zeros((rows_here, LANES), jnp.int16)
                    for phase in range(2):
                        scale_in[phase, k, n - 2] = jnp.zeros(scale_in.shape[3:], jnp.float32)
                    if dr == 0:
                        gside[k, 1 - s] = jnp.zeros(gside.shape[2:], jnp.int16)
                    else:
                        gcorner[k, 1 - s, 1 - u] = jnp.zeros(gcorner.shape[3:], jnp.int16)

    for h in range(homes):
        c = home_off[1, h] + (LANES - m)
        for at, value in enumerate((home_off[0, h], lax.div(c, LANES), lax.rem(c, LANES), h, 1)):
            meta[h, at] = jnp.int32(value)
    next_column = lax.rem(col + 1, n_col)
    rights, lefts = jnp.int32(0), jnp.int32(0)
    for h in range(slots):
        helper = helper_ref[h]
        live = jnp.where(helper >= 0, 1, 0)
        right = jnp.where(lax.rem(jnp.maximum(helper, 0), n_col) == next_column, live, 0)
        left = live - right
        held = jnp.minimum(right * rights + left * (half + lefts), slots - 1)
        rights, lefts = rights + right, lefts + left
        c = sur_off[1, h] + (LANES - m)
        values = (sur_off[0, h], lax.div(c, LANES), lax.rem(c, LANES), held, live)
        for at, value in enumerate(values):
            meta[homes + h, at] = value

    for a in range(2):
        for k in range(2):
            for q in range(inner):
                obj[k][a, 1 + q, m:m + tile, :] = x_ref[a, k, :, q * LANES:(q + 1) * LANES]
    patches[...] = jnp.zeros_like(patches)

    def unpack(k):
        wait_recv(halo_copies, k)
        lower, upper = (
            jnp.concatenate(
                [decode(side[k, s, edge(-dr, "ext")], 0, k, SIDES.index((dr, 1 - 2 * s))) for dr in (1, 0, -1)],
                axis=0,
            )
            for s in range(2)
        )
        obj[k][0, 0] = pltpu.roll(lower, LANES // 2, 1)
        obj[k][1, 0] = lower
        obj[k][0, tiles - 1] = upper
        obj[k][1, tiles - 1] = pltpu.roll(upper, LANES // 2, 1)

    lane = lanes((window, LANES))

    def cut(item, k):
        at, q, shift = meta[item, 0], meta[item, 1], meta[item, 2]
        out = []
        for a in range(2):
            here = obj[k][a, q, pl.ds(at, window), :]
            there = obj[k][a, q + 1, pl.ds(at, window), :]
            out.append(pltpu.roll(jnp.where(lane >= shift, here, there), LANES - shift, 1))
        return tuple(out)

    def put(item, grad):
        shift = meta[item, 2]
        for a in range(2):
            patches[item, a, tile:tile + window, :] = pltpu.roll(grad[a], shift, 1)

    def total(parts):
        return sum(p[0] for p in parts), sum(p[1] for p in parts)

    probes = lambda: [(probe_ref[0, j], probe_ref[1, j]) for j in range(modes)]
    kept = lambda item: [(waves[item, j, 0], waves[item, j, 1]) for j in range(modes)]

    def keep(item, fields):
        for j, (re, im) in enumerate(fields):
            waves[item, j, 0] = re
            waves[item, j, 1] = im

    def each(fn, begin=0):
        def step(i, carry):
            for j in range(GROUP):
                fn(i * GROUP + j)
            return carry

        lax.fori_loop(begin // GROUP, count // GROUP, step, 0)

    def enter(item):
        o1 = cut(item, 0)
        keep(item, sandwich([times(p, o1) for p in probes()], tab, 0, False))

    def middle(item, home=None):
        o2 = cut(item, 1)
        fields = kept(item)
        far = sandwich([times(b, o2) for b in fields], tab, 1, False)
        intensity = sum(re * re + im * im for re, im in far)
        amp = amps[meta[item, 3]] if home is None else home_amp[home]
        amp = amp.astype(jnp.float32)
        weight = 2.0 * meta[item, 4].astype(jnp.float32)
        factor = weight * (1.0 - amp * lax.rsqrt(intensity + EPS))
        exits = sandwich([(re * factor, im * factor) for re, im in far], tab, 1, True)
        put(item, total([conj_times(b, e) for b, e in zip(fields, exits)]))
        keep(item, [conj_times(o2, e) for e in exits])

    def leave(item):
        entry = sandwich(kept(item), tab, 0, True)
        put(item, total([conj_times(p, e) for p, e in zip(probes(), entry)]))

    chunk = 32

    def gather(k):
        lane8 = lanes((chunk, LANES))

        def step(i, carry):
            begin = pl.multiple_of(i * chunk, chunk)
            for a in range(2):
                sums = [jnp.zeros((chunk, LANES), jnp.float32) for _ in range(tiles)]
                for item in range(count):
                    at, q, shift = meta[item, 0], meta[item, 1], meta[item, 2]
                    piece = patches[item, a, pl.ds(tile - at + begin, chunk), :]
                    high = jnp.where(lane8 >= shift, piece, 0.0)
                    low = piece - high
                    for t in range(tiles):
                        hit = jnp.where(q == t, 1.0, 0.0)
                        miss = jnp.where(q + 1 == t, 1.0, 0.0)
                        sums[t] = sums[t] + (high * hit + low * miss)
                for t in range(tiles):
                    acc[a, k, t, pl.ds(begin, chunk), :] = sums[t]
            return carry

        lax.fori_loop(0, ext // chunk, step, 0)
        left = pair_up(acc[0, k, 0], acc[1, k, 0], True)
        right = pair_up(acc[0, k, tiles - 1], acc[1, k, tiles - 1], False)
        encode(gpack, 1, k, [left, right])
        start(grad_copies, k)

    def finish(k):
        wait_recv(grad_copies, k)
        low = lanes((tile, LANES)) < LANES // 2
        for q in range(inner):
            for a in range(2):
                value = acc[a, k, 1 + q, m:m + tile, :]
                top = value[:m] + grow[k, 0, a, q]
                bottom = value[tile - m:] + grow[k, 1, a, q]
                value = jnp.concatenate([top, value[m:tile - m], bottom], axis=0)
                for s in range(2):
                    if (s == 0 and q != 0) or (s == 1 and q != inner - 1):
                        continue
                    dc = 1 - 2 * s
                    extra = decode(gside[k, s], 1, k, SIDES.index((0, dc)))
                    top = decode(gcorner[k, s, 0], 1, k, SIDES.index((1, dc)))
                    bottom = decode(gcorner[k, s, 1], 1, k, SIDES.index((-1, dc)))
                    extra = jnp.concatenate(
                        [extra[:m] + top, extra[m:tile - m], extra[tile - m:] + bottom], axis=0
                    )
                    if a != s:
                        extra = pltpu.roll(extra, LANES // 2, 1)
                    value = value + jnp.where(low if s == 0 else jnp.logical_not(low), extra, 0.0)
                out_ref[a, k, :, q * LANES:(q + 1) * LANES] = value

    unpack(0)
    each(enter)
    unpack(1)
    for h in range(homes):
        middle(h, h)
    for copy in amp_copies:
        copy.wait_recv()
    each(middle, homes)
    gather(1)
    each(leave)
    gather(0)
    finish(1)
    finish(0)
    for k in range(2):
        wait_send(halo_copies, k)
        wait_send(grad_copies, k)
    for copy in amp_copies:
        copy.wait_send()


GROUP = 2


def shards(object_tiles, probe_modes, home_offset, home_amp, sur_offset, sur_helper, help_amp):
    window = probe_modes.shape[-1]
    modes = probe_modes.shape[1]
    tile = object_tiles.shape[-1]
    ext = tile + 2 * MARGIN
    tiles = tile // LANES + 2
    inner = tile // LANES
    count = home_amp.shape[2] + help_amp.shape[2]
    grid_shape = (lax.axis_size("row"), lax.axis_size("col"))
    vmem = pl.BlockSpec(memory_space=pltpu.VMEM)
    smem = pl.BlockSpec(memory_space=pltpu.SMEM)
    f32 = jnp.float32
    return pl.pallas_call(
        functools.partial(kernel, grid_shape),
        out_shape=jax.ShapeDtypeStruct(object_tiles.shape, f32),
        in_specs=[smem] * 3 + [vmem] * 5,
        out_specs=vmem,
        scratch_shapes=[
            pltpu.SMEM((count, 5), jnp.int32),
            pltpu.VMEM((2, tiles, ext, LANES), f32),
            pltpu.VMEM((2, tiles, ext, LANES), f32),
            pltpu.VMEM((2, 2, tiles, ext, LANES), f32),
            pltpu.VMEM((2, 2, tile, LANES), jnp.int16),
            pltpu.VMEM((2, 2, ext, LANES), jnp.int16),
            pltpu.VMEM((2, 2, ext, LANES), jnp.int16),
            pltpu.VMEM((2, 2, 2, inner, MARGIN, LANES), f32),
            pltpu.VMEM((2, 2, tile, LANES), jnp.int16),
            pltpu.VMEM((2, 2, 2, MARGIN, LANES), jnp.int16),
            pltpu.VMEM((2, 2, 8, LANES), f32),
            pltpu.VMEM((2, 2, 6, 8, LANES), f32),
            pltpu.VMEM((help_amp.shape[2], window, window), jnp.bfloat16),
            pltpu.VMEM((count, modes, 2, window, window), f32),
            pltpu.VMEM((count, 2, 2 * tile + window, LANES), f32),
            pltpu.SemaphoreType.DMA((2, 2, 8 + 8 * inner)),
            pltpu.SemaphoreType.DMA((2, 2, 8 + 8 * inner)),
            pltpu.SemaphoreType.DMA((2,)),
            pltpu.SemaphoreType.DMA((2,)),
        ],
        compiler_params=pltpu.CompilerParams(
            collective_id=0, has_side_effects=True, vmem_limit_bytes=60 << 20
        ),
        name="multislice",
    )(
        home_offset[0, 0], sur_offset[0, 0], sur_helper[0, 0],
        jnp.asarray(split_tables(window)), probe_modes, object_tiles, home_amp[0, 0], help_amp[0, 0],
    )


def solution(mesh):
    return jax.shard_map(
        shards,
        mesh=mesh,
        in_specs=(
            P(None, None, "row", "col"),
            P(),
            P("row", "col", None, None),
            P("row", "col", None, None, None),
            P("row", "col", None, None),
            P("row", "col", None),
            P("row", "col", None, None, None),
        ),
        out_specs=P(None, None, "row", "col"),
        check_vma=False,
    )
```

```python
import functools
import math

import numpy as np
import ml_dtypes
import jax
import jax.numpy as jnp
from jax import lax
from jax.experimental import pallas as pl
from jax.experimental.pallas import tpu as pltpu
from jax.sharding import PartitionSpec as P

MARGIN = 64
LANES = 128
EPS = 0.1
LEVELS = 32766.0
TINY = 1e-30
MESH = pl.DeviceIdType.MESH
SIDES = ((1, 0), (-1, 0), (0, 1), (0, -1), (1, 1), (-1, 1), (1, -1), (-1, -1))


def split_tables(window):
    index = np.arange(window)
    spectral = np.exp(-2j * np.pi / window * (index[:, None] * index[None, :] % window))
    spectral /= math.sqrt(window)
    freq = np.where(index >= window // 2, index - window, index).astype(np.float64)
    carrier = np.exp(-1j * np.pi / window * freq**2)
    propagate = np.conj(spectral) @ (carrier[:, None] * spectral)
    blocks = []
    for table in (propagate, spectral):
        blocks += [table.real, table.imag, -table.imag]
    full = np.stack(blocks).astype(np.float32)
    high = full.astype(ml_dtypes.bfloat16)
    low = (full - high.astype(np.float32)).astype(ml_dtypes.bfloat16)
    return np.stack([high, low])


def split(x):
    high = x.astype(jnp.bfloat16)
    low = (x - high.astype(jnp.float32)).astype(jnp.bfloat16)
    return high, low


def square(tab, which, flip):
    def one(part):
        re, im, neg = (tab[part, 3 * which + k] for k in range(3))
        if flip:
            im, neg = neg, im
        top = jnp.concatenate([re, im], axis=1)
        return jnp.concatenate([top, jnp.concatenate([neg, re], axis=1)], axis=0)

    return one(0), one(1)


def dot(a, b):
    return jnp.dot(a, b, preferred_element_type=jnp.float32)


def sandwich(fields, tab, which, conj):
    rows = [jnp.concatenate([re, im], axis=1) for re, im in fields]
    high, low = split(jnp.concatenate(rows, axis=0))
    t_high, t_low = square(tab, which, conj)
    first = dot(
        jnp.concatenate([high, low, high], axis=1),
        jnp.concatenate([t_high, t_high, t_low], axis=0),
    )
    w = first.shape[1] // 2
    count = len(fields)
    top = jnp.concatenate([first[m * w:(m + 1) * w, :w] for m in range(count)], axis=1)
    low_half = jnp.concatenate([first[m * w:(m + 1) * w, w:] for m in range(count)], axis=1)
    high, low = split(jnp.concatenate([top, low_half], axis=0))
    t_high, t_low = square(tab, which, not conj)
    second = dot(
        jnp.concatenate([t_high, t_low, t_high], axis=1),
        jnp.concatenate([high, high, low], axis=0),
    )
    return [
        (second[:w, m * w:(m + 1) * w], second[w:, m * w:(m + 1) * w]) for m in range(count)
    ]


def times(a, b):
    return a[0] * b[0] - a[1] * b[1], a[0] * b[1] + a[1] * b[0]


def conj_times(a, b):
    return a[0] * b[0] + a[1] * b[1], a[0] * b[1] - a[1] * b[0]


def lanes(shape):
    return lax.broadcasted_iota(jnp.int32, shape, len(shape) - 1)


def pair_up(re, im, keep_high):
    half = LANES // 2
    if keep_high:
        return jnp.where(lanes(re.shape) < half, pltpu.roll(re, half, 1), im)
    return jnp.where(lanes(re.shape) < half, re, pltpu.roll(im, half, 1))


def kernel(
    grid_shape, home_off, sur_off, helper_ref, tab, probe_ref, x_ref, home_amp, help_amp, out_ref,
    meta, obj0, obj1, acc, pack, side, gpack, grow, gside, gcorner, scale_out, scale_in, amps, waves, patches, masks,
    send_sem, recv_sem, amp_send, amp_recv,
):
    n_row, n_col = grid_shape
    obj = (obj0, obj1)
    row, col = lax.axis_index("row"), lax.axis_index("col")
    tile = x_ref.shape[2]
    window = probe_ref.shape[-1]
    modes = probe_ref.shape[1]
    homes = home_amp.shape[0]
    slots = help_amp.shape[0]
    half = slots // 2
    count = homes + slots
    m = MARGIN
    ext = tile + 2 * m
    tiles = obj0.shape[1]
    inner = tile // LANES

    def inside(dr, dc):
        r, c = row + dr, col + dc
        return (r >= 0) & (r < n_row) & (c >= 0) & (c < n_col)

    ring = [(row, lax.rem(col + 1, n_col)), (row, lax.rem(col + n_col - 1, n_col))]
    barrier = pltpu.get_barrier_semaphore()
    for target in ring:
        pl.semaphore_signal(barrier, inc=1, device_id=target, device_id_type=MESH)
    for dr, dc in SIDES:
        if dr != 0:
            @pl.when(inside(dr, dc))
            def _(dr=dr, dc=dc):
                pl.semaphore_signal(
                    barrier, inc=1, device_id=(row + dr, col + dc), device_id_type=MESH
                )

    def encode(target, phase, k, strips):
        top = functools.reduce(
            jnp.maximum, [jnp.max(jnp.abs(v), axis=(0, 1), keepdims=True) for v in strips]
        )
        top = jnp.maximum(top, TINY)
        for s, v in enumerate(strips):
            target[k, s] = jnp.round(v * (LEVELS / top)).astype(jnp.int32).astype(jnp.int16)
        scale_out[phase, k] = jnp.broadcast_to(top * (1.0 / LEVELS), scale_out.shape[2:])

    def decode(value, phase, k, n):
        return value.astype(jnp.int32).astype(jnp.float32) * scale_in[phase, k, n - 2, 0:1, :]

    for k in range(2):
        first, last = x_ref[:, k, :, 0:LANES], x_ref[:, k, :, tile - LANES:tile]
        encode(pack, 0, k, [pair_up(first[0], first[1], False), pair_up(last[0], last[1], True)])

    vertical = jnp.where(row > 0, 1, 0) + jnp.where(row + 1 < n_row, 1, 0)
    across = 1 + jnp.where(col > 0, 1, 0) + jnp.where(col + 1 < n_col, 1, 0)
    pl.semaphore_wait(barrier, 2 + vertical * across)

    def remote(src, dst, phase, k, index, target):
        return pltpu.make_async_remote_copy(
            src_ref=src, dst_ref=dst,
            send_sem=send_sem.at[phase, k, index], recv_sem=recv_sem.at[phase, k, index],
            device_id=target, device_id_type=MESH,
        )

    def edge(d, source):
        if d == 0:
            return slice(m, m + tile) if source == "ext" else slice(0, tile)
        if source == "ext":
            return slice(ext - m, ext) if d > 0 else slice(0, m)
        return slice(tile - m, tile) if d > 0 else slice(0, m)

    def scale_copy(phase, k, n, target):
        return remote(
            scale_out.at[phase, k], scale_in.at[phase, k, n - 2], phase, k, 8 * inner + n, target
        )

    def halo_copies(n, k):
        dr, dc = SIDES[n]
        target = (row + dr, col + dc)
        landing = edge(-dr, "ext")
        if dc == 0:
            return [
                remote(
                    x_ref.at[:, k, edge(dr, "tile"), q * LANES:(q + 1) * LANES],
                    obj[k].at[:, 1 + q, landing, :], 0, k, n + 8 * q, target,
                )
                for q in range(inner)
            ]
        s = 1 if dc > 0 else 0
        return [
            remote(pack.at[k, s, edge(dr, "tile")], side.at[k, 1 - s, landing], 0, k, n, target),
            scale_copy(0, k, n, target),
        ]

    def grad_copies(n, k):
        dr, dc = SIDES[n]
        target = (row + dr, col + dc)
        take = edge(dr, "ext")
        if dc == 0:
            u = 1 if dr > 0 else 0
            return [remote(acc.at[:, k, 1:1 + inner, take, :], grow.at[k, 1 - u], 1, k, n, target)]
        s = 1 if dc > 0 else 0
        source = gpack.at[k, s, take]
        if dr == 0:
            landing = gside.at[k, 1 - s]
        else:
            landing = gcorner.at[k, 1 - s, 0 if dr > 0 else 1]
        return [remote(source, landing, 1, k, n, target), scale_copy(1, k, n, target)]

    def start(copies, k):
        for n, (dr, dc) in sorted(enumerate(SIDES), key=lambda e: e[1][1] == 0):
            @pl.when(inside(dr, dc))
            def _(n=n):
                for copy in copies(n, k):
                    copy.start()

    def wait_recv(copies, k):
        for n, (dr, dc) in enumerate(SIDES):
            @pl.when(inside(-dr, -dc))
            def _(n=n):
                for copy in copies(n, k):
                    copy.wait_recv()

    def wait_send(copies, k):
        for n, (dr, dc) in enumerate(SIDES):
            @pl.when(inside(dr, dc))
            def _(n=n):
                for copy in copies(n, k):
                    copy.wait_send()

    start(halo_copies, 0)
    start(halo_copies, 1)
    amp_copies = [
        pltpu.make_async_remote_copy(
            src_ref=help_amp.at[h * half:(h + 1) * half],
            dst_ref=amps.at[h * half:(h + 1) * half],
            send_sem=amp_send.at[h], recv_sem=amp_recv.at[h],
            device_id=ring[1 - h], device_id_type=MESH,
        )
        for h in range(2)
    ]
    for copy in amp_copies:
        copy.start()

    for n, (dr, dc) in enumerate(SIDES):
        @pl.when(jnp.logical_not(inside(-dr, -dc)))
        def _(n=n, dr=dr, dc=dc):
            landing = edge(-dr, "ext")
            u = 1 if dr > 0 else 0
            s = 1 if dc > 0 else 0
            for k in range(2):
                if dc == 0:
                    halo = obj[k][:, 1:1 + inner, landing, :]
                    obj[k][:, 1:1 + inner, landing, :] = jnp.zeros(halo.shape, jnp.float32)
                    grow[k, 1 - u] = jnp.zeros(grow.shape[2:], jnp.float32)
                else:
                    rows_here = landing.stop - landing.start
                    side[k, 1 - s, landing] = jnp.zeros((rows_here, LANES), jnp.int16)
                    for phase in range(2):
                        scale_in[phase, k, n - 2] = jnp.zeros(scale_in.shape[3:], jnp.float32)
                    if dr == 0:
                        gside[k, 1 - s] = jnp.zeros(gside.shape[2:], jnp.int16)
                    else:
                        gcorner[k, 1 - s, 1 - u] = jnp.zeros(gcorner.shape[3:], jnp.int16)

    for h in range(homes):
        c = home_off[1, h] + (LANES - m)
        for at, value in enumerate((home_off[0, h], lax.div(c, LANES), lax.rem(c, LANES), h, 1)):
            meta[h, at] = jnp.int32(value)
    next_column = lax.rem(col + 1, n_col)
    rights, lefts = jnp.int32(0), jnp.int32(0)
    for h in range(slots):
        helper = helper_ref[h]
        live = jnp.where(helper >= 0, 1, 0)
        right = jnp.where(lax.rem(jnp.maximum(helper, 0), n_col) == next_column, live, 0)
        left = live - right
        held = jnp.minimum(right * rights + left * (half + lefts), slots - 1)
        rights, lefts = rights + right, lefts + left
        c = sur_off[1, h] + (LANES - m)
        values = (sur_off[0, h], lax.div(c, LANES), lax.rem(c, LANES), held, live)
        for at, value in enumerate(values):
            meta[homes + h, at] = value

    for a in range(2):
        for k in range(2):
            for q in range(inner):
                obj[k][a, 1 + q, m:m + tile, :] = x_ref[a, k, :, q * LANES:(q + 1) * LANES]
    patches[...] = jnp.zeros_like(patches)
    lane8 = lanes((8, LANES))
    for item in range(count):
        begin = meta[item, 1] * LANES + meta[item, 2]
        for t in range(tiles):
            d = lane8 + (t * LANES - begin)
            masks[item, t] = jnp.where((d >= 0) & (d < LANES), 1.0, 0.0)

    def unpack(k):
        wait_recv(halo_copies, k)
        lower, upper = (
            jnp.concatenate(
                [decode(side[k, s, edge(-dr, "ext")], 0, k, SIDES.index((dr, 1 - 2 * s))) for dr in (1, 0, -1)],
                axis=0,
            )
            for s in range(2)
        )
        obj[k][0, 0] = pltpu.roll(lower, LANES // 2, 1)
        obj[k][1, 0] = lower
        obj[k][0, tiles - 1] = upper
        obj[k][1, tiles - 1] = pltpu.roll(upper, LANES // 2, 1)

    lane = lanes((window, LANES))

    def cut(item, k):
        at, q, shift = meta[item, 0], meta[item, 1], meta[item, 2]
        out = []
        for a in range(2):
            here = obj[k][a, q, pl.ds(at, window), :]
            there = obj[k][a, q + 1, pl.ds(at, window), :]
            out.append(pltpu.roll(jnp.where(lane >= shift, here, there), LANES - shift, 1))
        return tuple(out)

    def put(item, grad):
        shift = meta[item, 2]
        for a in range(2):
            patches[item, a, tile:tile + window, :] = pltpu.roll(grad[a], shift, 1)

    def total(parts):
        return sum(p[0] for p in parts), sum(p[1] for p in parts)

    probes = lambda: [(probe_ref[0, j], probe_ref[1, j]) for j in range(modes)]
    kept = lambda item: [(waves[item, j, 0], waves[item, j, 1]) for j in range(modes)]

    def keep(item, fields):
        for j, (re, im) in enumerate(fields):
            waves[item, j, 0] = re
            waves[item, j, 1] = im

    def each(fn, begin=0):
        group = next(g for g in SIZES if (count - begin) % g == 0)

        def step(i, carry):
            fn([begin + i * group + j for j in range(group)])
            return carry

        lax.fori_loop(0, (count - begin) // group, step, 0)

    def joint(groups, which, conj):
        flat = sandwich([f for fields in groups for f in fields], tab, which, conj)
        return [flat[i * modes:(i + 1) * modes] for i in range(len(groups))]

    def enter(items):
        waves_in = []
        for item in items:
            o1 = cut(item, 0)
            waves_in.append([times(p, o1) for p in probes()])
        for item, fields in zip(items, joint(waves_in, 0, False)):
            keep(item, fields)

    def middle(items, home=False):
        o2s = [cut(item, 1) for item in items]
        fields = [[times(b, o2) for b in kept(item)] for item, o2 in zip(items, o2s)]
        seen = []
        for item, far in zip(items, joint(fields, 1, False)):
            intensity = sum(re * re + im * im for re, im in far)
            amp = home_amp[item] if home else amps[meta[item, 3]]
            weight = 2.0 * meta[item, 4].astype(jnp.float32)
            factor = weight * (1.0 - amp.astype(jnp.float32) * lax.rsqrt(intensity + EPS))
            seen.append([(re * factor, im * factor) for re, im in far])
        for item, o2, exits in zip(items, o2s, joint(seen, 1, True)):
            put(item, total([conj_times(b, e) for b, e in zip(kept(item), exits)]))
            keep(item, [conj_times(o2, e) for e in exits])

    def leave(items):
        for item, entry in zip(items, joint([kept(item) for item in items], 0, True)):
            put(item, total([conj_times(p, e) for p, e in zip(probes(), entry)]))

    chunk = 32

    def gather(k):
        def step(i, carry):
            begin = pl.multiple_of(i * chunk, chunk)
            for a in range(2):
                sums = [jnp.zeros((chunk, LANES), jnp.float32) for _ in range(tiles)]
                for item in range(count):
                    piece = patches[item, a, pl.ds(tile - meta[item, 0] + begin, chunk), :]
                    for t in range(tiles):
                        mask = jnp.concatenate([masks[item, t]] * (chunk // 8), axis=0)
                        sums[t] = sums[t] + piece * mask
                for t in range(tiles):
                    acc[a, k, t, pl.ds(begin, chunk), :] = sums[t]
            return carry

        lax.fori_loop(0, ext // chunk, step, 0)
        left = pair_up(acc[0, k, 0], acc[1, k, 0], True)
        right = pair_up(acc[0, k, tiles - 1], acc[1, k, tiles - 1], False)
        encode(gpack, 1, k, [left, right])
        start(grad_copies, k)

    def finish(k):
        wait_recv(grad_copies, k)
        low = lanes((tile, LANES)) < LANES // 2
        for q in range(inner):
            for a in range(2):
                value = acc[a, k, 1 + q, m:m + tile, :]
                top = value[:m] + grow[k, 0, a, q]
                bottom = value[tile - m:] + grow[k, 1, a, q]
                value = jnp.concatenate([top, value[m:tile - m], bottom], axis=0)
                for s in range(2):
                    if (s == 0 and q != 0) or (s == 1 and q != inner - 1):
                        continue
                    dc = 1 - 2 * s
                    extra = decode(gside[k, s], 1, k, SIDES.index((0, dc)))
                    top = decode(gcorner[k, s, 0], 1, k, SIDES.index((1, dc)))
                    bottom = decode(gcorner[k, s, 1], 1, k, SIDES.index((-1, dc)))
                    extra = jnp.concatenate(
                        [extra[:m] + top, extra[m:tile - m], extra[tile - m:] + bottom], axis=0
                    )
                    if a != s:
                        extra = pltpu.roll(extra, LANES // 2, 1)
                    value = value + jnp.where(low if s == 0 else jnp.logical_not(low), extra, 0.0)
                out_ref[a, k, :, q * LANES:(q + 1) * LANES] = value

    unpack(0)
    each(enter)
    unpack(1)
    middle(list(range(homes)), True)
    for copy in amp_copies:
        copy.wait_recv()
    each(middle, homes)
    gather(1)
    each(leave)
    gather(0)
    finish(1)
    finish(0)
    for k in range(2):
        wait_send(halo_copies, k)
        wait_send(grad_copies, k)
    for copy in amp_copies:
        copy.wait_send()


SIZES = (4, 3, 2, 1)


def shards(object_tiles, probe_modes, home_offset, home_amp, sur_offset, sur_helper, help_amp):
    window = probe_modes.shape[-1]
    modes = probe_modes.shape[1]
    tile = object_tiles.shape[-1]
    ext = tile + 2 * MARGIN
    tiles = tile // LANES + 2
    inner = tile // LANES
    count = home_amp.shape[2] + help_amp.shape[2]
    grid_shape = (lax.axis_size("row"), lax.axis_size("col"))
    vmem = pl.BlockSpec(memory_space=pltpu.VMEM)
    smem = pl.BlockSpec(memory_space=pltpu.SMEM)
    f32 = jnp.float32
    return pl.pallas_call(
        functools.partial(kernel, grid_shape),
        out_shape=jax.ShapeDtypeStruct(object_tiles.shape, f32),
        in_specs=[smem] * 3 + [vmem] * 5,
        out_specs=vmem,
        scratch_shapes=[
            pltpu.SMEM((count, 5), jnp.int32),
            pltpu.VMEM((2, tiles, ext, LANES), f32),
            pltpu.VMEM((2, tiles, ext, LANES), f32),
            pltpu.VMEM((2, 2, tiles, ext, LANES), f32),
            pltpu.VMEM((2, 2, tile, LANES), jnp.int16),
            pltpu.VMEM((2, 2, ext, LANES), jnp.int16),
            pltpu.VMEM((2, 2, ext, LANES), jnp.int16),
            pltpu.VMEM((2, 2, 2, inner, MARGIN, LANES), f32),
            pltpu.VMEM((2, 2, tile, LANES), jnp.int16),
            pltpu.VMEM((2, 2, 2, MARGIN, LANES), jnp.int16),
            pltpu.VMEM((2, 2, 8, LANES), f32),
            pltpu.VMEM((2, 2, 6, 8, LANES), f32),
            pltpu.VMEM((help_amp.shape[2], window, window), jnp.bfloat16),
            pltpu.VMEM((count, modes, 2, window, window), f32),
            pltpu.VMEM((count, 2, 2 * tile + window, LANES), f32),
            pltpu.VMEM((count, tiles, 8, LANES), f32),
            pltpu.SemaphoreType.DMA((2, 2, 8 + 8 * inner)),
            pltpu.SemaphoreType.DMA((2, 2, 8 + 8 * inner)),
            pltpu.SemaphoreType.DMA((2,)),
            pltpu.SemaphoreType.DMA((2,)),
        ],
        compiler_params=pltpu.CompilerParams(
            collective_id=0, has_side_effects=True, vmem_limit_bytes=60 << 20
        ),
        name="multislice",
    )(
        home_offset[0, 0], sur_offset[0, 0], sur_helper[0, 0],
        jnp.asarray(split_tables(window)), probe_modes, object_tiles, home_amp[0, 0], help_amp[0, 0],
    )


def solution(mesh):
    return jax.shard_map(
        shards,
        mesh=mesh,
        in_specs=(
            P(None, None, "row", "col"),
            P(),
            P("row", "col", None, None),
            P("row", "col", None, None, None),
            P("row", "col", None, None),
            P("row", "col", None),
            P("row", "col", None, None, None),
        ),
        out_specs=P(None, None, "row", "col"),
        check_vma=False,
    )
```
